32 devices in a mesh: tm: 16 (over z, y, x), row: 2 (over core).
Axes of the slice: x: 2, y: 2, z: 4, core: 2. Of those that a mesh axis runs over, the one named last changes fastest.
Arguments:
- transition: bfloat16 [16, 896, 896], P('tm', 'row'), as said below
- offsets: float32 [16, 896, 128], P('tm', 'row'), may hold values from -0.72 to 0.72
- start: float32 [896, 128], P('row'), may hold values from -6 to 6
Outputs:
- states: float32 [16, 896, 128], P('tm', 'row')
The draws below stay inside these ranges and needn't reach their ends.
Inputs may be any that keep to these rules, and one draw needn't show every extreme that they name: The products of consecutive transition matrices stay bounded.
All inputs are finite; a program needn't handle non-finite values.
Results may differ from the reference program's by a relative error of at most 0.0003.
Values sent between devices are 32-bit elements; how exact they have to be, the bound alone decides.
No kernel may reach another device: no remote copies, remote signals or barrier semaphores. Data moves between devices by JAX's collectives and lax.ppermute only.
A program may use at most 64 MiB of HBM per device.

```python
import math
import jax
import jax.numpy as jnp
from jax import lax

NS = 896
COLS = 128
TIME_SLICES = 16


def draw_transition(key, part):
    angle_key = jax.random.fold_in(key, 21)
    rate_key = jax.random.fold_in(key, 22)
    jitter_key = jax.random.fold_in(key, 23)
    spike_random_key = jax.random.fold_in(key, 24)
    factor_key = jax.random.fold_in(key, 25)
    dense_key = jax.random.fold_in(key, 26)
    worker_units = NS // 2
    growth_rates = jnp.exp(jax.random.uniform(rate_key, (1, worker_units), jnp.float32, math.log(0.3), math.log(5.0)))
    angles = jax.random.uniform(angle_key, (TIME_SLICES, worker_units), jnp.float32, 0.05, 1.2)
    spread = 0.1
    random_perturbation = jax.random.uniform(jitter_key, (TIME_SLICES, worker_units), jnp.float32, 0.5, 1.5)
    spike_slice_list = jax.random.randint(spike_random_key, (3, worker_units), 0, TIME_SLICES)
    spike_mask = jnp.any(spike_slice_list[:, None, :] == jnp.arange(TIME_SLICES)[None, :, None], axis=0)
    decay_losses = jax.random.uniform(factor_key, (TIME_SLICES, worker_units), jnp.float32, 0.55, 0.85)
    wrap_divisor = jnp.exp(-growth_rates * random_perturbation / TIME_SLICES) * jnp.where(spike_mask, decay_losses, jnp.float32(1.0))
    cosine = jnp.repeat(wrap_divisor * jnp.cos(angles), 2, axis=1)
    sine_part = jnp.repeat(wrap_divisor * jnp.sin(angles), 2, axis=1)
    parity = jnp.arange(NS) % 2
    upper_band = jnp.eye(NS, k=1, dtype=jnp.float32) * (parity == 0).astype(jnp.float32)[:, None]
    lower_band = jnp.eye(NS, k=-1, dtype=jnp.float32) * (parity == 1).astype(jnp.float32)[:, None]
    identity = jnp.eye(NS, dtype=jnp.float32)
    dense_part = jax.random.normal(dense_key, (TIME_SLICES, NS, NS), jnp.float32) * (spread / NS ** 0.5)
    complete = dense_part + identity[None, :, :] * cosine[:, :, None]
    complete = complete + (upper_band - lower_band)[None, :, :] * sine_part[:, :, None]
    return complete.astype(jnp.bfloat16)


def shard_levels(own_key, dims, cuts, smallest, top_value):
    def one(position, shards_of):
        heights = jax.random.uniform(jax.random.fold_in(jax.random.fold_in(own_key, 6), position), (shards_of,), jnp.float32, smallest / len(cuts), top_value / len(cuts))
        return jnp.repeat(jnp.exp(heights), dims[position] // shards_of).reshape((-1,) + (1,) * (len(dims) - position - 1))

    level = one(*cuts[0])
    for cut in cuts[1:]:
        level = level * one(*cut)
    return level


def centred(key, shape, deviation, reach, shards=(), kind=jnp.bfloat16):
    drawn = jax.random.normal(key, shape, jnp.float32) * deviation
    if len(shards) > 0:
        drawn = shard_levels(key, shape, shards, -0.22, 0.18) * drawn
    return jnp.clip(drawn, min=-reach, max=reach).astype(kind)


def setup_inputs(seed: int = 0) -> dict:
    key_of = jax.random.split(jax.random.key(seed), 4)
    return {
        "transition": draw_transition(jax.random.fold_in(key_of[3], 71), 0),
        "offsets": centred(key_of[1], (TIME_SLICES, NS, COLS), 0.12, 0.72, ((0, 16), (1, 2)), jnp.float32),
        "start": centred(key_of[2], (NS, COLS), 1.0, 6.0, ((0, 2),), jnp.float32),
    }


def reference(transition, offsets, start):
    def advance(current, pieces):
        matrix, offset = pieces
        current = jnp.dot(matrix.astype(jnp.float32), current, precision=lax.Precision.HIGHEST) + offset
        return current, current

    last_state, states = lax.scan(advance, start.astype(jnp.float32), (transition, offsets))
    return states
```

```python
import functools

import jax
import jax.numpy as jnp
from jax import lax
from jax.experimental import pallas as pl
from jax.experimental.pallas import tpu as pltpu
from jax.sharding import PartitionSpec as P

CHUNKS = 2
VMEM = pltpu.VMEM


def swap_cores(block):
    n = lax.axis_size("row")
    return lax.ppermute(block, "row", [(i, (i + 1) % n) for i in range(n)])


def hop(block, stage):
    slices, rows = lax.axis_size("tm"), lax.axis_size("row")
    route = []
    for i in range(slices):
        to = {stage: stage + 1, stage + 1: stage}.get(i)
        for r in range(rows):
            target = (i, (r + 1) % rows) if to is None else (to, r)
            route.append((i * rows + r, target[0] * rows + target[1]))
    return lax.ppermute(block, ("tm", "row"), route)


def matrix_kernel(mine_ref, other_ref, out_ref):
    first = lax.axis_index("row") == 0
    mine = mine_ref[...].astype(jnp.float32)
    other = other_ref[...]
    top = jnp.where(first, mine, other)
    low = jnp.where(first, other, mine)
    whole = jnp.concatenate([top, low], axis=0)
    out_ref[...] = whole.T.astype(jnp.bfloat16)


def stage_kernel(stage, x_ref, matrix_ref, offset_ref, before_ref, y_ref):
    del before_ref

    @pl.when(lax.axis_index("tm") == stage)
    def _():
        x = x_ref[...]
        rows = x.shape[0]
        high = x.astype(jnp.bfloat16)
        low = (x - high.astype(jnp.float32)).astype(jnp.bfloat16)
        both = jnp.concatenate([high, low], axis=0)
        product = jnp.dot(both, matrix_ref[...], preferred_element_type=jnp.float32)
        y_ref[...] = product[:rows] + product[rows:] + offset_ref[...]


def stage_call(stage, x, matrix, offset, y):
    spec = pl.BlockSpec(memory_space=VMEM)
    rows, order = x.shape
    return pl.pallas_call(
        functools.partial(stage_kernel, stage),
        out_shape=jax.ShapeDtypeStruct(x.shape, jnp.float32),
        in_specs=[spec] * 4,
        out_specs=spec,
        input_output_aliases={3: 0},
        compiler_params=pltpu.CompilerParams(vmem_limit_bytes=8 << 20),
        cost_estimate=pl.CostEstimate(
            flops=4 * rows * order * order, bytes_accessed=2 * order * order, transcendentals=0
        ),
        name="stage",
    )(x, matrix, offset, y)


def local(transition, offsets, start):
    slices = lax.axis_size("tm")
    row = lax.axis_index("row")
    own = transition[0]
    part, order = own.shape
    columns = start.shape[1]
    half = columns // lax.axis_size("row")
    chunk = half // CHUNKS

    spec = pl.BlockSpec(memory_space=VMEM)
    other = swap_cores(own.astype(jnp.float32))
    matrix = pl.pallas_call(
        matrix_kernel,
        out_shape=jax.ShapeDtypeStruct((order, order), jnp.bfloat16),
        in_specs=[spec] * 2,
        out_specs=spec,
        compiler_params=pltpu.CompilerParams(vmem_limit_bytes=24 << 20),
        name="matrix",
    )(own, other)

    rows_t = jnp.stack([start.T, offsets[0].T])
    keep = lax.dynamic_slice_in_dim(rows_t, row * half, half, axis=1)
    give = lax.dynamic_slice_in_dim(rows_t, (1 - row) * half, half, axis=1)
    got = swap_cores(give)
    whole = jnp.where(
        row == 0,
        jnp.concatenate([keep, got], axis=2),
        jnp.concatenate([got, keep], axis=2),
    )
    xs = [whole[0, c * chunk : (c + 1) * chunk] for c in range(CHUNKS)]
    bs = [whole[1, c * chunk : (c + 1) * chunk] for c in range(CHUNKS)]
    ys = [jnp.zeros_like(b) for b in bs]
    for stage in range(slices):
        for c in range(CHUNKS):
            ys[c] = stage_call(stage, xs[c], matrix, bs[c], ys[c])
            if stage + 1 < slices:
                xs[c] = hop(ys[c], stage)
    result = jnp.concatenate(ys, axis=0)
    mine = lax.dynamic_slice_in_dim(result, row * part, part, axis=1)
    give = lax.dynamic_slice_in_dim(result, (1 - row) * part, part, axis=1)
    got = swap_cores(give)
    out_t = jnp.where(
        row == 0,
        jnp.concatenate([mine, got], axis=0),
        jnp.concatenate([got, mine], axis=0),
    )
    return out_t.T[None]


def solution(mesh):
    in_specs = (P("tm", "row", None), P("tm", "row", None), P("row", None))
    out_specs = P("tm", "row", None)
    return jax.shard_map(local, mesh=mesh, in_specs=in_specs, out_specs=out_specs, check_vma=False)
```

```python
import functools

import jax
import jax.numpy as jnp
from jax import lax
from jax.experimental import pallas as pl
from jax.experimental.pallas import tpu as pltpu
from jax.sharding import PartitionSpec as P


CHUNKS = 2
SINGLE = 8
ANY = pl.BlockSpec(memory_space=pl.ANY)
HBM = pl.BlockSpec(memory_space=pltpu.HBM)
VMEM = pl.BlockSpec(memory_space=pltpu.VMEM)
F32, BF16 = jnp.float32, jnp.bfloat16


def route_of(to, spare):
    slices, rows = lax.axis_size("tm"), lax.axis_size("row")
    route = []
    for i in range(slices):
        for r in range(rows):
            if i in to:
                route.append((i * rows + r, to[i] * rows + r))
            elif spare:
                route.append((i * rows + r, i * rows + (r + 1) % rows))
    return route


def hop(block, pairs):
    to = {}
    for a, b in pairs:
        to[a], to[b] = b, a
    return lax.ppermute(block, ("tm", "row"), route_of(to, True))


def ship(block, evens):
    return lax.ppermute(block, ("tm", "row"), route_of({e: e + 1 for e in evens}, False))


def swap_cores(block, places=None):
    rows = lax.axis_size("row")
    places = range(lax.axis_size("tm")) if places is None else places
    route = [(i * rows + r, i * rows + (r + 1) % rows) for i in places for r in range(rows)]
    return lax.ppermute(block, ("tm", "row"), route)


def call(kernel, operands, specs, outs, aliases=None, flops=0, limit=8, scratch=()):
    moved = sum(o.size * o.dtype.itemsize for o in outs)
    return pl.pallas_call(
        kernel,
        out_shape=tuple(outs),
        in_specs=specs,
        out_specs=tuple([VMEM] * len(outs)),
        scratch_shapes=scratch,
        input_output_aliases=aliases or {},
        compiler_params=pltpu.CompilerParams(vmem_limit_bytes=limit << 20),
        cost_estimate=pl.CostEstimate(flops=flops, bytes_accessed=moved, transcendentals=0),
    )(*operands)


def gate(block, *after):
    def kernel(*refs):
        del refs

    return pl.pallas_call(
        kernel,
        out_shape=jax.ShapeDtypeStruct(block.shape, block.dtype),
        in_specs=[ANY] * (1 + len(after)),
        out_specs=ANY,
        input_output_aliases={0: 0},
        compiler_params=pltpu.CompilerParams(vmem_limit_bytes=1 << 20),
        name="gate",
    )(block, *after)


def is_any(places):
    here = lax.axis_index("tm")
    found = here == places[0]
    for place in places[1:]:
        found = jnp.logical_or(found, here == place)
    return found


def first_core():
    return lax.axis_index("row") == 0


def both_halves(mine, other):
    first = first_core()
    return jnp.concatenate(
        [jnp.where(first, mine, other), jnp.where(first, other, mine)], axis=0
    )


def own_columns(mine, other):
    across = both_halves(mine, other).T
    half = mine.shape[1] // 2
    return jnp.where(first_core(), across[:half], across[half:])


def split_product(x, matrix):
    rows = x.shape[0]
    high = x.astype(BF16)
    low = (x - high.astype(F32)).astype(BF16)
    product = jnp.dot(
        jnp.concatenate([high, low], axis=0), matrix, preferred_element_type=F32
    )
    return product[:rows] + product[rows:]


def first_kernel(own_ref, offset_ref, start_ref, other_start_ref, keep_ref, give_ref):
    @pl.when(is_any([0]))
    def _():
        x = both_halves(start_ref[...], other_start_ref[...]).T
        high = x.astype(BF16)
        low = (x - high.astype(F32)).astype(BF16)
        across = (((1,), (1,)), ((), ()))
        y = lax.dot_general(high, own_ref[...], across, preferred_element_type=F32)
        y += lax.dot_general(low, own_ref[...], across, preferred_element_type=F32)
        y += offset_ref[...].T
        half = y.shape[0] // 2
        first = first_core()
        keep_ref[...] = jnp.where(first, y[:half], y[half:])
        give_ref[...] = jnp.where(first, y[half:], y[:half])


def join_kernel(keep_ref, got_ref, *y_refs):
    @pl.when(is_any([0]))
    def _():
        first = first_core()
        keep, got = keep_ref[...], got_ref[...]
        y = jnp.concatenate(
            [jnp.where(first, keep, got), jnp.where(first, got, keep)], axis=1
        )
        chunk = y_refs[0].shape[0]
        for c in range(CHUNKS):
            y_refs[c][...] = y[c * chunk : (c + 1) * chunk]


def begin_kernel(own_ref, offset_ref, other_ref, other_offset_ref, matrix_ref, columns_ref):
    own = own_ref[...].astype(F32)
    matrix_ref[...] = both_halves(own, other_ref[...]).T.astype(BF16)
    columns_ref[...] = own_columns(offset_ref[...], other_offset_ref[...])


def migrate_kernel(odds, own_ref, other_ref, matrix_ref):
    @pl.when(is_any(odds))
    def _():
        matrix_ref[...] = both_halves(own_ref[...], other_ref[...]).T.astype(BF16)


def step_kernel(c, plan, alias, x_refs, matrix_ref, offset_ref, got_ref, got_offset_ref, before_ref, y_ref):
    chunk = y_ref.shape[0]
    here = pl.ds(c * chunk, chunk)
    everyone = [place for places in plan.values() for place in places]
    for (source, double), places in plan.items():

        @pl.when(is_any(places))
        def _(source=source, double=double):
            x = x_refs[source][...]
            if double:
                x = split_product(x, got_ref[...]) + got_offset_ref[here]
            y_ref[...] = split_product(x, matrix_ref[...]) + offset_ref[here]

    if not alias:

        @pl.when(jnp.logical_not(is_any(everyone)))
        def _():
            y_ref[...] = before_ref[...]


def local(transition, offsets, start):
    slices = lax.axis_size("tm")
    own, offset = transition[0], offsets[0]
    part, order = own.shape
    columns = start.shape[1]
    half = columns // 2
    chunk = half // CHUNKS
    shape = jax.ShapeDtypeStruct
    piece = shape((chunk, order), F32)
    evens = list(range(SINGLE, slices, 2))
    odds = [e + 1 for e in evens]
    product = 4 * chunk * order * order

    block = shape((half, part), F32)
    other_start = swap_cores(start)
    wide = own.astype(F32)
    shipped = ship(wide, evens)
    keep, give = call(
        first_kernel, (own, offset, start, other_start), [VMEM] * 4, [block] * 2,
        flops=4 * columns * part * order, limit=16,
    )
    got = swap_cores(give)
    ys = list(call(join_kernel, (keep, got), [VMEM] * 2, [piece] * CHUNKS))
    other = swap_cores(wide)
    other_offset = swap_cores(offset)
    matrix, offset = call(
        begin_kernel, (own, offset, other, other_offset), [VMEM] * 4,
        [shape((order, order), BF16), shape((half, order), F32)], limit=24,
    )
    got_offset = ship(offset, evens)

    def step(c, xs, plan, got=(), after=(), alias=True):
        double = len(got) > 0
        count = len(xs)

        def kernel(*refs):
            x_refs, refs = refs[:count], refs[count:]
            before_ref, matrix_ref, offset_ref = refs[:3]
            got_ref, got_offset_ref = refs[3:5] if double else (None, None)
            step_kernel(c, plan, alias, x_refs, matrix_ref, offset_ref, got_ref, got_offset_ref, before_ref, refs[-1])

        after = (ys[c - 1], *after)
        (ys[c],) = call(
            kernel,
            (*xs, ys[c], matrix, offset, *got, *after),
            [VMEM] * (count + 3 + len(got)) + [ANY] * len(after), [piece],
            aliases={count: 0} if alias else None, flops=product * (1 + double),
        )

    def move(c, pairs):
        return hop(ys[c], pairs)

    for stage in range(1, SINGLE):
        if stage == SINGLE - 1:
            shipped = gate(shipped, *ys)
            shipped_other = swap_cores(shipped)
            (moved,) = call(
                functools.partial(migrate_kernel, odds), (shipped, shipped_other), [VMEM] * 2,
                [shape((order, order), BF16)], limit=24,
            )
        for c in range(CHUNKS):
            x = move(c, [(stage - 1, stage)])
            step(c, [x], {(0, False): [stage]})
    for odd in odds:
        last = odd == slices - 1
        pairs = [(odd - 2, odd)] + ([(odd - 4, odd - 3)] if odd > odds[0] else [])
        plan = {(0, True): [odd]}
        if odd > odds[0]:
            plan[(0, False)] = [odd - 3]
        if last:
            plan[(1, False)] = [odd - 1]
        for c in range(CHUNKS):
            xs = [move(c, pairs)] + ([move(c, [(odd - 2, odd - 1)])] if last else [])
            step(c, xs, plan, got=(moved, got_offset), alias=not last)

    def give_kernel(*refs):
        y = jnp.concatenate([ref[...] for ref in refs[:CHUNKS]], axis=0)
        refs[-1][...] = jnp.where(first_core(), y[:, part:], y[:, :part])

    def end_kernel(*refs):
        y = jnp.concatenate([ref[...] for ref in refs[:CHUNKS]], axis=0)
        first = first_core()
        mine = jnp.where(first, y[:, :part], y[:, part:])
        taken = refs[CHUNKS][...]
        rows = jnp.concatenate(
            [jnp.where(first, mine, taken), jnp.where(first, taken, mine)], axis=0
        )
        refs[-1][...] = rows.T

    (give,) = call(give_kernel, tuple(ys), [VMEM] * CHUNKS, [shape((half, part), F32)])
    (out,) = call(
        end_kernel, (*ys, swap_cores(give)), [VMEM] * (CHUNKS + 1), [shape((part, columns), F32)]
    )
    return out[None]


def solution(mesh):
    in_specs = (P("tm", "row", None), P("tm", "row", None), P("row", None))
    out_specs = P("tm", "row", None)
    return jax.shard_map(local, mesh=mesh, in_specs=in_specs, out_specs=out_specs, check_vma=False)
```

```python
import functools

import jax
import jax.numpy as jnp
from jax import lax
from jax.experimental import pallas as pl
from jax.experimental.pallas import tpu as pltpu
from jax.sharding import PartitionSpec as P


CHUNKS = 2
SINGLE = 8
ANY = pl.BlockSpec(memory_space=pl.ANY)
HBM = pl.BlockSpec(memory_space=pltpu.HBM)
VMEM = pl.BlockSpec(memory_space=pltpu.VMEM)
F32, BF16 = jnp.float32, jnp.bfloat16


def route_of(to, spare):
    slices, rows = lax.axis_size("tm"), lax.axis_size("row")
    route = []
    for i in range(slices):
        for r in range(rows):
            if i in to:
                route.append((i * rows + r, to[i] * rows + r))
            elif spare:
                route.append((i * rows + r, i * rows + (r + 1) % rows))
    return route


def hop(block, *cycles):
    to = {}
    for cycle in cycles:
        to.update(zip(cycle, cycle[1:] + cycle[:1]))
    return lax.ppermute(block, ("tm", "row"), route_of(to, True))


def ship(block, evens):
    return lax.ppermute(block, ("tm", "row"), route_of({e: e + 1 for e in evens}, False))


def swap_cores(block, places=None):
    rows = lax.axis_size("row")
    places = range(lax.axis_size("tm")) if places is None else places
    route = [(i * rows + r, i * rows + (r + 1) % rows) for i in places for r in range(rows)]
    return lax.ppermute(block, ("tm", "row"), route)


def call(kernel, operands, specs, outs, aliases=None, flops=0, limit=8, scratch=()):
    moved = sum(o.size * o.dtype.itemsize for o in outs)
    return pl.pallas_call(
        kernel,
        out_shape=tuple(outs),
        in_specs=specs,
        out_specs=tuple([VMEM] * len(outs)),
        scratch_shapes=scratch,
        input_output_aliases=aliases or {},
        compiler_params=pltpu.CompilerParams(vmem_limit_bytes=limit << 20),
        cost_estimate=pl.CostEstimate(flops=flops, bytes_accessed=moved, transcendentals=0),
    )(*operands)


def gate(block, *after):
    def kernel(*refs):
        del refs

    return pl.pallas_call(
        kernel,
        out_shape=jax.ShapeDtypeStruct(block.shape, block.dtype),
        in_specs=[ANY] * (1 + len(after)),
        out_specs=ANY,
        input_output_aliases={0: 0},
        compiler_params=pltpu.CompilerParams(vmem_limit_bytes=1 << 20),
        name="gate",
    )(block, *after)


def is_any(places):
    here = lax.axis_index("tm")
    found = here == places[0]
    for place in places[1:]:
        found = jnp.logical_or(found, here == place)
    return found


def first_core():
    return lax.axis_index("row") == 0


def both_halves(mine, other):
    first = first_core()
    return jnp.concatenate(
        [jnp.where(first, mine, other), jnp.where(first, other, mine)], axis=0
    )


def own_columns(mine, other):
    across = both_halves(mine, other).T
    half = mine.shape[1] // 2
    return jnp.where(first_core(), across[:half], across[half:])


def split_product(x, matrix):
    rows = x.shape[0]
    high = x.astype(BF16)
    low = (x - high.astype(F32)).astype(BF16)
    product = jnp.dot(
        jnp.concatenate([high, low], axis=0), matrix, preferred_element_type=F32
    )
    return product[:rows] + product[rows:]


def first_kernel(own_ref, offset_ref, start_ref, other_start_ref, keep_ref, give_ref):
    @pl.when(is_any([0]))
    def _():
        x = both_halves(start_ref[...], other_start_ref[...]).T
        high = x.astype(BF16)
        low = (x - high.astype(F32)).astype(BF16)
        across = (((1,), (1,)), ((), ()))
        y = lax.dot_general(high, own_ref[...], across, preferred_element_type=F32)
        y += lax.dot_general(low, own_ref[...], across, preferred_element_type=F32)
        y += offset_ref[...].T
        half = y.shape[0] // 2
        first = first_core()
        keep_ref[...] = jnp.where(first, y[:half], y[half:])
        give_ref[...] = jnp.where(first, y[half:], y[:half])


def join_kernel(keep_ref, got_ref, *y_refs):
    @pl.when(is_any([0]))
    def _():
        first = first_core()
        keep, got = keep_ref[...], got_ref[...]
        y = jnp.concatenate(
            [jnp.where(first, keep, got), jnp.where(first, got, keep)], axis=1
        )
        chunk = y_refs[0].shape[0]
        for c in range(CHUNKS):
            y_refs[c][...] = y[c * chunk : (c + 1) * chunk]


def begin_kernel(own_ref, offset_ref, other_ref, other_offset_ref, matrix_ref, columns_ref):
    own = own_ref[...].astype(F32)
    matrix_ref[...] = both_halves(own, other_ref[...]).T.astype(BF16)
    columns_ref[...] = own_columns(offset_ref[...], other_offset_ref[...])


def migrate_kernel(odds, own_ref, other_ref, matrix_ref):
    @pl.when(is_any(odds))
    def _():
        matrix_ref[...] = both_halves(own_ref[...], other_ref[...]).T.astype(BF16)


def step_kernel(c, plan, alias, x_refs, matrix_ref, offset_ref, got_ref, got_offset_ref, before_ref, y_ref):
    chunk = y_ref.shape[0]
    here = pl.ds(c * chunk, chunk)
    everyone = [place for places in plan.values() for place in places]
    for (source, double), places in plan.items():

        @pl.when(is_any(places))
        def _(source=source, double=double):
            x = x_refs[source][...]
            if double:
                x = split_product(x, got_ref[...]) + got_offset_ref[here]
            y_ref[...] = split_product(x, matrix_ref[...]) + offset_ref[here]

    if not alias:

        @pl.when(jnp.logical_not(is_any(everyone)))
        def _():
            y_ref[...] = before_ref[...]


def local(transition, offsets, start):
    slices = lax.axis_size("tm")
    own, offset = transition[0], offsets[0]
    part, order = own.shape
    columns = start.shape[1]
    half = columns // 2
    chunk = half // CHUNKS
    shape = jax.ShapeDtypeStruct
    piece = shape((chunk, order), F32)
    evens = list(range(SINGLE, slices, 2))
    odds = [e + 1 for e in evens]
    product = 4 * chunk * order * order

    block = shape((half, part), F32)
    other_start = swap_cores(start)
    wide = own.astype(F32)
    shipped = ship(wide, evens)
    keep, give = call(
        first_kernel, (own, offset, start, other_start), [VMEM] * 4, [block] * 2,
        flops=4 * columns * part * order, limit=16,
    )
    got = swap_cores(give)
    ys = list(call(join_kernel, (keep, got), [VMEM] * 2, [piece] * CHUNKS))
    other = swap_cores(wide)
    other_offset = swap_cores(offset)
    matrix, offset = call(
        begin_kernel, (own, offset, other, other_offset), [VMEM] * 4,
        [shape((order, order), BF16), shape((half, order), F32)], limit=24,
    )
    got_offset = ship(offset, evens)

    def step(c, xs, plan, got=(), after=(), alias=True):
        double = len(got) > 0
        count = len(xs)

        def kernel(*refs):
            x_refs, refs = refs[:count], refs[count:]
            before_ref, matrix_ref, offset_ref = refs[:3]
            got_ref, got_offset_ref = refs[3:5] if double else (None, None)
            step_kernel(c, plan, alias, x_refs, matrix_ref, offset_ref, got_ref, got_offset_ref, before_ref, refs[-1])

        after = (ys[c - 1], *after)
        (ys[c],) = call(
            kernel,
            (*xs, ys[c], matrix, offset, *got, *after),
            [VMEM] * (count + 3 + len(got)) + [ANY] * len(after), [piece],
            aliases={count: 0} if alias else None, flops=product * (1 + double),
        )

    def move(c, *cycles):
        return hop(ys[c], *cycles)

    for stage in range(1, SINGLE):
        for c in range(CHUNKS):
            x = move(c, (stage - 1, stage))
            step(c, [x], {(0, False): [stage]})
            if (stage, c) == (SINGLE - 1, 0):
                shipped = gate(shipped, ys[c])
                shipped_other = swap_cores(shipped)
                (moved,) = call(
                    functools.partial(migrate_kernel, odds), (shipped, shipped_other), [VMEM] * 2,
                    [shape((order, order), BF16)], limit=24,
                )
    for odd in odds:
        last = odd == slices - 1
        cycles = [(odd - 2, odd, *([odd - 8] if odd == odds[0] else []))] + ([(odd - 4, odd - 3, odd - (5 if last else 11))] if odd > odds[0] else [])
        plan = {(0, True): [odd]}
        if odd > odds[0]:
            plan[(0, False)] = [odd - 3]
        if last:
            plan[(1, False)] = [odd - 1]
        for c in range(CHUNKS):
            xs = [move(c, *cycles)] + ([move(c, (odd - 2, odd - 1, odd - 7))] if last else [])
            step(c, xs, plan, got=(moved, got_offset), alias=not last)

    def give_kernel(*refs):
        y = jnp.concatenate([ref[...] for ref in refs[:CHUNKS]], axis=0)
        refs[-1][...] = jnp.where(first_core(), y[:, part:], y[:, :part])

    def end_kernel(*refs):
        y = jnp.concatenate([ref[...] for ref in refs[:CHUNKS]], axis=0)
        first = first_core()
        mine = jnp.where(first, y[:, :part], y[:, part:])
        taken = refs[CHUNKS][...]
        rows = jnp.concatenate(
            [jnp.where(first, mine, taken), jnp.where(first, taken, mine)], axis=0
        )
        refs[-1][...] = rows.T

    (give,) = call(give_kernel, tuple(ys), [VMEM] * CHUNKS, [shape((half, part), F32)])
    (out,) = call(end_kernel, (*ys, swap_cores(give)), [VMEM] * (CHUNKS + 1), [shape((part, columns), F32)])
    return out[None]


def solution(mesh):
    in_specs = (P("tm", "row", None), P("tm", "row", None), P("row", None))
    out_specs = P("tm", "row", None)
    return jax.shard_map(local, mesh=mesh, in_specs=in_specs, out_specs=out_specs, check_vma=False)
```

```python
import functools

import jax
import jax.numpy as jnp
from jax import lax
from jax.experimental import pallas as pl
from jax.experimental.pallas import tpu as pltpu
from jax.sharding import PartitionSpec as P


CHUNKS = 2
SINGLE = 8
ANY = pl.BlockSpec(memory_space=pl.ANY)
HBM = pl.BlockSpec(memory_space=pltpu.HBM)
VMEM = pl.BlockSpec(memory_space=pltpu.VMEM)
F32, BF16 = jnp.float32, jnp.bfloat16


def route_of(to, spare):
    slices, rows = lax.axis_size("tm"), lax.axis_size("row")
    route = []
    for i in range(slices):
        for r in range(rows):
            if i in to:
                route.append((i * rows + r, to[i] * rows + r))
            elif spare:
                route.append((i * rows + r, i * rows + (r + 1) % rows))
    return route


def hop(block, *cycles):
    to = {}
    for cycle in cycles:
        to.update(zip(cycle, cycle[1:] + cycle[:1]))
    return lax.ppermute(block, ("tm", "row"), route_of(to, True))


def ship(block, evens):
    return lax.ppermute(block, ("tm", "row"), route_of({e: e + 1 for e in evens}, False))


def swap_cores(block, places=None):
    rows = lax.axis_size("row")
    places = range(lax.axis_size("tm")) if places is None else places
    route = [(i * rows + r, i * rows + (r + 1) % rows) for i in places for r in range(rows)]
    return lax.ppermute(block, ("tm", "row"), route)


def call(kernel, operands, specs, outs, aliases=None, flops=0, limit=8, scratch=()):
    moved = sum(o.size * o.dtype.itemsize for o in outs)
    return pl.pallas_call(
        kernel,
        out_shape=tuple(outs),
        in_specs=specs,
        out_specs=tuple([VMEM] * len(outs)),
        scratch_shapes=scratch,
        input_output_aliases=aliases or {},
        compiler_params=pltpu.CompilerParams(vmem_limit_bytes=limit << 20),
        cost_estimate=pl.CostEstimate(flops=flops, bytes_accessed=moved, transcendentals=0),
    )(*operands)


def gate(block, *after):
    def kernel(*refs):
        del refs

    return pl.pallas_call(
        kernel,
        out_shape=jax.ShapeDtypeStruct(block.shape, block.dtype),
        in_specs=[ANY] * (1 + len(after)),
        out_specs=ANY,
        input_output_aliases={0: 0},
        compiler_params=pltpu.CompilerParams(vmem_limit_bytes=1 << 20),
        name="gate",
    )(block, *after)


def is_any(places):
    here = lax.axis_index("tm")
    found = here == places[0]
    for place in places[1:]:
        found = jnp.logical_or(found, here == place)
    return found


def first_core():
    return lax.axis_index("row") == 0


def both_halves(mine, other):
    first = first_core()
    return jnp.concatenate(
        [jnp.where(first, mine, other), jnp.where(first, other, mine)], axis=0
    )


def own_columns(mine, other):
    across = both_halves(mine, other).T
    half = mine.shape[1] // 2
    return jnp.where(first_core(), across[:half], across[half:])


def split_product(x, matrix):
    rows = x.shape[0]
    high = x.astype(BF16)
    low = (x - high.astype(F32)).astype(BF16)
    product = jnp.dot(
        jnp.concatenate([high, low], axis=0), matrix, preferred_element_type=F32
    )
    return product[:rows] + product[rows:]


def first_kernel(own_ref, offset_ref, start_ref, other_start_ref, keep_ref, give_ref):
    @pl.when(is_any([0]))
    def _():
        x = both_halves(start_ref[...], other_start_ref[...]).T
        high = x.astype(BF16)
        low = (x - high.astype(F32)).astype(BF16)
        across = (((1,), (1,)), ((), ()))
        y = lax.dot_general(high, own_ref[...], across, preferred_element_type=F32)
        y += lax.dot_general(low, own_ref[...], across, preferred_element_type=F32)
        y += offset_ref[...].T
        half = y.shape[0] // 2
        first = first_core()
        keep_ref[...] = jnp.where(first, y[:half], y[half:])
        give_ref[...] = jnp.where(first, y[half:], y[:half])


def join_kernel(keep_ref, got_ref, *y_refs):
    @pl.when(is_any([0]))
    def _():
        first = first_core()
        keep, got = keep_ref[...], got_ref[...]
        y = jnp.concatenate(
            [jnp.where(first, keep, got), jnp.where(first, got, keep)], axis=1
        )
        chunk = y_refs[0].shape[0]
        for c in range(CHUNKS):
            y_refs[c][...] = y[c * chunk : (c + 1) * chunk]


def begin_kernel(own_ref, offset_ref, other_ref, other_offset_ref, matrix_ref, columns_ref):
    own = own_ref[...].astype(F32)
    matrix_ref[...] = both_halves(own, other_ref[...]).T.astype(BF16)
    columns_ref[...] = own_columns(offset_ref[...], other_offset_ref[...])


def migrate_kernel(odds, own_ref, other_ref, matrix_ref):
    @pl.when(is_any(odds))
    def _():
        matrix_ref[...] = both_halves(own_ref[...], other_ref[...]).T.astype(BF16)


def step_kernel(c, plan, alias, x_refs, matrix_ref, offset_ref, got_ref, got_offset_ref, before_ref, y_ref):
    chunk = y_ref.shape[0]
    here = pl.ds(c * chunk, chunk)
    everyone = [place for places in plan.values() for place in places]
    for (source, double), places in plan.items():

        @pl.when(is_any(places))
        def _(source=source, double=double):
            x = x_refs[source][...]
            if double:
                x = split_product(x, got_ref[...]) + got_offset_ref[here]
            y_ref[...] = split_product(x, matrix_ref[...]) + offset_ref[here]

    if not alias:

        @pl.when(jnp.logical_not(is_any(everyone)))
        def _():
            y_ref[...] = before_ref[...]


def local(transition, offsets, start):
    slices = lax.axis_size("tm")
    own, offset = transition[0], offsets[0]
    part, order = own.shape
    columns = start.shape[1]
    half = columns // 2
    chunk = half // CHUNKS
    shape = jax.ShapeDtypeStruct
    piece = shape((chunk, order), F32)
    evens = list(range(SINGLE, slices, 2))
    odds = [e + 1 for e in evens]
    product = 4 * chunk * order * order

    block = shape((half, part), F32)
    other_start = swap_cores(start)
    wide = own.astype(F32)
    shipped = ship(wide, evens)
    keep, give = call(
        first_kernel, (own, offset, start, other_start), [VMEM] * 4, [block] * 2,
        flops=4 * columns * part * order, limit=16,
    )
    got = swap_cores(give)
    ys = list(call(join_kernel, (keep, got), [VMEM] * 2, [piece] * CHUNKS))
    other = swap_cores(wide)
    other_offset = swap_cores(offset)
    matrix, offset = call(
        begin_kernel, (own, offset, other, other_offset), [VMEM] * 4,
        [shape((order, order), BF16), shape((half, order), F32)], limit=24,
    )
    got_offset = ship(offset, evens)

    gives = []

    def step(c, xs, plan, got=(), after=(), alias=True):
        double = len(got) > 0
        count = len(xs)

        def kernel(*refs):
            x_refs, refs = refs[:count], refs[count:]
            before_ref, matrix_ref, offset_ref = refs[:3]
            got_ref, got_offset_ref = refs[3:5] if double else (None, None)
            step_kernel(c, plan, alias, x_refs, matrix_ref, offset_ref, got_ref, got_offset_ref, before_ref, refs[-1 - len(gave)])
            if gave:
                y_ref, first = refs[-2], first_core()
                refs[-1][...] = jnp.where(first, y_ref[:, part:], y_ref[:, :part])

        gave = [] if alias else [shape((chunk, part), F32)]
        after = (ys[c - 1], *after)
        ys[c], *sent = call(
            kernel,
            (*xs, ys[c], matrix, offset, *got, *after),
            [VMEM] * (count + 3 + len(got)) + [ANY] * len(after), [piece, *gave],
            aliases={count: 0} if alias else None, flops=product * (1 + double),
        )
        gives.extend(sent)

    def move(c, *cycles):
        return hop(ys[c], *cycles)

    for stage in range(1, SINGLE):
        for c in range(CHUNKS):
            x = move(c, (stage - 1, stage))
            step(c, [x], {(0, False): [stage]})
            if (stage, c) == (SINGLE - 1, 0):
                shipped = gate(shipped, ys[c])
                shipped_other = swap_cores(shipped)
                (moved,) = call(
                    functools.partial(migrate_kernel, odds), (shipped, shipped_other), [VMEM] * 2,
                    [shape((order, order), BF16)], limit=24,
                )
    for odd in odds:
        last = odd == slices - 1
        cycles = [(odd - 2, odd, *([odd - 8] if odd == odds[0] else []))] + ([(odd - 4, odd - 3, odd - (5 if last else 11))] if odd > odds[0] else [])
        plan = {(0, True): [odd]}
        if odd > odds[0]:
            plan[(0, False)] = [odd - 3]
        if last:
            plan[(1, False)] = [odd - 1]
        for c in range(CHUNKS):
            xs = [move(c, *cycles)] + ([move(c, (odd - 2, odd - 1, odd - 7))] if last else [])
            step(c, xs, plan, got=(moved, got_offset), alias=not last)

    def end_kernel(*refs):
        y = jnp.concatenate([ref[...] for ref in refs[:CHUNKS]], axis=0)
        first = first_core()
        mine = jnp.where(first, y[:, :part], y[:, part:])
        taken = jnp.concatenate([ref[...] for ref in refs[CHUNKS:-1]], axis=0)
        rows = jnp.concatenate(
            [jnp.where(first, mine, taken), jnp.where(first, taken, mine)], axis=0
        )
        refs[-1][...] = rows.T

    (out,) = call(end_kernel, (*ys, *map(swap_cores, gives)), [VMEM] * (2 * CHUNKS), [shape((part, columns), F32)])
    return out[None]


def solution(mesh):
    in_specs = (P("tm", "row", None), P("tm", "row", None), P("row", None))
    out_specs = P("tm", "row", None)
    return jax.shard_map(local, mesh=mesh, in_specs=in_specs, out_specs=out_specs, check_vma=False)
```
